32 devices in a mesh: strip: 8 (over z, y), panel: 4 (over x, core).
Axes of the slice: x: 2, y: 2, z: 4, core: 2. Of those that a mesh axis runs over, the one named last changes fastest.
Arguments:
- h_cond: float32 [32, 256], P('strip', 'panel'), may hold values from 0.3 to 3
- v_cond: float32 [32, 256], P('strip', 'panel'), may hold values from 0.3 to 3
- confidence: float32 [32, 256], P('strip', 'panel'), may hold values from 1.8e-05 to 0.00225
- teacher: float32 [16, 32, 256], P(None, 'strip', 'panel'), may hold values from -6 to 6
- grad_x: float32 [16, 32, 256], P(None, 'strip', 'panel'), may hold values from -4 to 4
- grad_y: float32 [16, 32, 256], P(None, 'strip', 'panel'), may hold values from -4 to 4
Outputs:
- depth: float32 [16, 32, 256], P(None, 'strip', 'panel')
The draws below stay inside these ranges and needn't reach their ends.
All inputs are finite; a program needn't handle non-finite values.
Results may differ from the reference program's by a relative error of at most 0.0003.
Values sent between devices are 32-bit elements; how exact they have to be, the bound alone decides.
A program may use at most 320 MiB of HBM per device.

```python
import math
import jax
import jax.numpy as jnp
from jax import lax

LON = 256
ROWS_DEV = 4
MAPS = 16
ROWS = 32


def smooth_field(key, leading):
    subkeys = jax.random.split(key, 6)
    polarity = (jax.random.randint(subkeys[0], (leading, 3), 0, 2) * 2 - 1).astype(jnp.float32)
    amplitude = jax.random.uniform(subkeys[1], (leading, 3), jnp.float32, 0.5, 1.0) * polarity
    row_freq = jax.random.uniform(subkeys[2], (leading, 3), jnp.float32, 0.3, 1.5)
    col_freq = jax.random.randint(subkeys[3], (leading, 3), 0, 3).astype(jnp.float32)
    row_phase = jax.random.uniform(subkeys[4], (leading, 3), jnp.float32, 0.0, 2.0 * math.pi)
    col_phase = jax.random.uniform(subkeys[5], (leading, 3), jnp.float32, 0.0, 2.0 * math.pi)
    row_pos = jnp.arange(ROWS, dtype=jnp.float32) / ROWS
    col_pos = jnp.arange(LON, dtype=jnp.float32) / LON
    row_wave = jnp.cos(2.0 * math.pi * row_freq[:, :, None] * row_pos[None, None, :] + row_phase[:, :, None])
    col_wave = jnp.cos(2.0 * math.pi * col_freq[:, :, None] * col_pos[None, None, :] + col_phase[:, :, None])
    pattern = jnp.sum(amplitude[:, :, None, None] * row_wave[:, :, :, None] * col_wave[:, :, None, :], axis=1)
    return pattern / jnp.sum(jnp.abs(amplitude), axis=1)[:, None, None]


def draw_confidence(key, part):
    key = jax.random.fold_in(key, 11)
    smooth_key, rough_key = jax.random.split(key)
    smooth = smooth_field(smooth_key, 1)[0]
    rough = jax.random.uniform(rough_key, (ROWS, LON), jnp.float32, -1.0, 1.0)
    return 0.0003 * jnp.exp(1.2 * smooth + 0.8 * rough)


def draw_teacher(key, part):
    key = jax.random.fold_in(key, 23)
    smooth_key, rough_key = jax.random.split(key)
    smooth = smooth_field(smooth_key, MAPS)
    rough = jax.random.truncated_normal(rough_key, -4.0, 4.0, (MAPS, ROWS, LON), jnp.float32)
    return rough + 2.0 * smooth


def block_scale(stream_key, shape, cuts, least, top_value):
    gain = 1.0
    for axis_at, blocks in cuts:
        draws = jax.random.uniform(jax.random.fold_in(jax.random.fold_in(stream_key, 6), axis_at), (blocks,), jnp.float32, least / len(cuts), top_value / len(cuts))
        gain = gain * jnp.repeat(jnp.exp(draws), shape[axis_at] // blocks).reshape((-1,) + (1,) * (len(shape) - 1 - axis_at))
    return gain


def centred(stream_key, shape, spread, bound, cuts=(), held_as=jnp.bfloat16):
    array = spread * jax.random.normal(stream_key, shape, jnp.float32)
    if cuts:
        array = array * block_scale(stream_key, shape, cuts, -0.22, 0.18)
    return jnp.clip(array, -bound, bound).astype(held_as)


def setup_inputs(seed: int = 0) -> dict:
    splits = jax.random.split(jax.random.key(seed), 7)
    return {
        "h_cond": jnp.clip(jnp.exp(math.log(3.0) - 2.3025851 * jax.random.uniform(splits[0], (ROWS, LON), jnp.float32) ** block_scale(splits[0], (ROWS, LON), ((0, 8), (1, 4)), -0.2, 0.2)), 0.3, 3.0),
        "v_cond": jnp.clip(jnp.exp(math.log(3.0) - 2.3025851 * jax.random.uniform(splits[1], (ROWS, LON), jnp.float32) ** block_scale(splits[1], (ROWS, LON), ((0, 8), (1, 4)), -0.2, 0.2)), 0.3, 3.0),
        "confidence": draw_confidence(jax.random.fold_in(splits[6], 71), 0),
        "teacher": draw_teacher(jax.random.fold_in(splits[6], 71), 0),
        "grad_x": centred(splits[4], (MAPS, ROWS, LON), 0.5, 4.0, ((1, 8), (2, 4)), jnp.float32),
        "grad_y": centred(splits[5], (MAPS, ROWS, LON), 0.5, 4.0, ((1, 8), (2, 4)), jnp.float32),
    }


HIGH = lax.Precision.HIGHEST

def product(left, right):
    return jnp.dot(left.astype(jnp.float32), right.astype(jnp.float32), precision=HIGH, preferred_element_type=jnp.float32)

def apply_to(matrix, vectors):
    return product(vectors, matrix.T)

def row_matrix(diag_row, link_row):
    extent = diag_row.shape[0]
    row_ids = lax.broadcasted_iota(jnp.int32, (extent, extent), 0)
    col_ids = lax.broadcasted_iota(jnp.int32, (extent, extent), 1)
    east = col_ids == (row_ids + 1) % extent
    west = row_ids == (col_ids + 1) % extent
    link = jnp.where(east, link_row[:, None], 0.0) + jnp.where(west, link_row[None, :], 0.0)
    return jnp.where(row_ids == col_ids, diag_row[:, None], 0.0) - link

def inverse(matrix):
    factor = jnp.linalg.cholesky(matrix)
    return jax.scipy.linalg.cho_solve((factor, True), jnp.eye(matrix.shape[0], dtype=jnp.float32))

def reference(h_cond, v_cond, confidence, teacher, grad_x, grad_y):
    rows, extent = h_cond.shape
    hypotheses = teacher.shape[0]
    zero_row = jnp.zeros((1, extent), jnp.float32)
    vertical_above = jnp.concatenate([zero_row, v_cond[:-1]], axis=0)
    flux = v_cond[None] * grad_y
    flux_above = jnp.concatenate([jnp.zeros((hypotheses, 1, extent), jnp.float32), flux[:, :-1]], axis=1)
    along = h_cond[None] * grad_x
    loads = confidence[None] * teacher + jnp.roll(along, 1, axis=2) - along + flux_above - flux
    loads = jnp.transpose(loads, (1, 0, 2))
    diagonal = jnp.roll(h_cond, 1, axis=1) + h_cond + vertical_above + v_cond + confidence
    span = ROWS_DEV * 8
    count = rows // span
    diag_b = diagonal.reshape(count, span, extent)
    link_b = h_cond.reshape(count, span, extent)
    above_b = vertical_above.reshape(count, span, extent)
    load_b = loads.reshape(count, span, hypotheses, extent)
    below_b = v_cond.reshape(count, span, extent)

    def advance(state, inputs):
        inverse_prev, load_prev = state
        diag_row, link_row, coupling, load_row = inputs
        pivot = row_matrix(diag_row, link_row) - coupling[:, None] * inverse_prev * coupling[None, :]
        carried = load_row + coupling[None, :] * apply_to(inverse_prev, load_prev)
        inverse_now = inverse(pivot)
        return ((inverse_now, carried), (inverse_now, carried))
    start = (jnp.eye(extent, dtype=jnp.float32), jnp.zeros((hypotheses, extent), jnp.float32))

    def block_pass(state, block_inputs):
        final, _ = lax.scan(advance, state, block_inputs)
        return (final, state)
    _, starts = lax.scan(block_pass, start, (diag_b, link_b, above_b, load_b))

    def block_back(value_below, block_inputs):
        start_state, diag_rows, link_rows, above_rows, load_rows, below_rows = block_inputs
        _, (inverses, carried) = lax.scan(advance, start_state, (diag_rows, link_rows, above_rows, load_rows))

        def back_row(value_next, inputs):
            inverse_row, carried_row, coupling_below = inputs
            value = apply_to(inverse_row, carried_row + coupling_below[None, :] * value_next)
            return (value, value)
        first_value, values = lax.scan(back_row, value_below, (inverses, carried, below_rows), reverse=True)
        return (first_value, values)
    _, depth = lax.scan(block_back, jnp.zeros((hypotheses, extent), jnp.float32), (starts, diag_b, link_b, above_b, load_b, below_b), reverse=True)
    return jnp.transpose(depth.reshape(rows, hypotheses, extent), (1, 0, 2))
```

```python
import functools

import jax
import jax.numpy as jnp
from jax import lax
from jax.experimental import pallas as pl
from jax.experimental.pallas import tpu as pltpu
from jax.sharding import PartitionSpec as P

HIGH = lax.Precision.HIGHEST


def shifted(value, axis, by):
    count = lax.axis_size(axis)
    pairs = [(i, i + by) for i in range(count) if 0 <= i + by < count]
    return lax.ppermute(value, axis, pairs)


def carried_in(value, axis, join, neutral, backward):
    count, mine = (lax.axis_size(axis), lax.axis_index(axis))
    pieces = jax.tree.map(lambda part: lax.all_gather(part, axis), value)
    if backward:
        pieces = jax.tree.map(lambda part: part[::-1], pieces)
        mine = count - 1 - mine
    total = jax.tree.map(
        lambda part, zero: jnp.full_like(part, 0) + jnp.asarray(zero, part.dtype), value, neutral
    )

    def turn(position, total):
        longer = join(total, jax.tree.map(lambda part: part[position], pieces))
        return jax.tree.map(lambda new, old: jnp.where(position < mine, new, old), longer, total)

    return lax.fori_loop(0, count - 1, turn, total)


def product(left, right):
    return jnp.dot(left, right, precision=HIGH, preferred_element_type=jnp.float32)


def apply_to(matrix, vectors):
    return product(vectors, matrix.T)


def row_matrix(diag_row, link_row):
    extent = diag_row.shape[0]
    row_ids = lax.broadcasted_iota(jnp.int32, (extent, extent), 0)
    col_ids = lax.broadcasted_iota(jnp.int32, (extent, extent), 1)
    east = col_ids == (row_ids + 1) % extent
    west = row_ids == (col_ids + 1) % extent
    link = jnp.where(east, link_row[:, None], 0.0) + jnp.where(west, link_row[None, :], 0.0)
    return jnp.where(row_ids == col_ids, diag_row[:, None], 0.0) - link


def inverse(matrix):
    factor = jnp.linalg.cholesky(matrix)
    return jax.scipy.linalg.cho_solve((factor, True), jnp.eye(matrix.shape[0], dtype=jnp.float32))


def load_update(factor, upper, lower):
    vector = jax.scipy.linalg.cho_solve((factor, True), (upper[4] + lower[3]).T)
    return (upper[3] - product(upper[1], vector).T, lower[4] - product(lower[1].T, vector).T)


def merge_whole(upper, lower):
    extent = upper[2].shape[0]
    factor = jnp.linalg.cholesky(upper[2] + lower[0])
    solved = jax.scipy.linalg.cho_solve(
        (factor, True), jnp.concatenate([upper[1].T, lower[1]], axis=1)
    )
    first_cols = solved[:, :extent]
    second_cols = solved[:, extent:]
    first_load, second_load = load_update(factor, upper, lower)
    return (
        upper[0] - product(upper[1], first_cols),
        -product(upper[1], second_cols),
        lower[2] - product(lower[1].T, second_cols),
        first_load,
        second_load,
    )


def merge_flagged(upper, lower):
    merged = merge_whole(upper[:5], lower[:5])
    upper_empty = upper[5] > 0.5
    lower_empty = lower[5] > 0.5
    picked = tuple(
        (
            jnp.where(upper_empty, lower_part, jnp.where(lower_empty, upper_part, merged_part))
            for upper_part, lower_part, merged_part in zip(upper[:5], lower[:5], merged)
        )
    )
    return picked + (upper[5] * lower[5],)


def chain_maps(earlier_map, later_map):
    return (
        product(later_map[0], earlier_map[0]),
        later_map[1] + apply_to(later_map[0], earlier_map[1]),
    )


def substitute(value_below, inputs):
    gain, offset = inputs
    value = offset + apply_to(gain, value_below)
    return (value, value)


def latitude_shards(h_cond, v_cond, confidence, teacher, grad_x, grad_y):
    slice_cols = h_cond.shape[1]
    local_rows = h_cond.shape[0]
    hypotheses = teacher.shape[0]
    edge_rows = jnp.concatenate([v_cond[-1][None], v_cond[-1][None] * grad_y[:, -1]], axis=0)
    above = shifted(edge_rows, "strip", 1)
    packed = jnp.concatenate(
        [
            h_cond,
            v_cond,
            confidence,
            above,
            teacher.reshape(hypotheses * local_rows, slice_cols),
            grad_x.reshape(hypotheses * local_rows, slice_cols),
            grad_y.reshape(hypotheses * local_rows, slice_cols),
        ],
        axis=0,
    )
    whole = lax.all_gather(packed, "panel", axis=1, tiled=True)
    extent = whole.shape[1]
    horizontal = whole[:local_rows]
    vertical = whole[local_rows : 2 * local_rows]
    weights = whole[2 * local_rows : 3 * local_rows]
    vertical_edge = whole[3 * local_rows]
    flux_edge = whole[3 * local_rows + 1 : 3 * local_rows + 1 + hypotheses]
    base = 3 * local_rows + 1 + hypotheses
    stride = hypotheses * local_rows
    targets = whole[base : base + stride].reshape(hypotheses, local_rows, extent)
    slope_x = whole[base + stride : base + 2 * stride].reshape(hypotheses, local_rows, extent)
    slope_y = whole[base + 2 * stride : base + 3 * stride].reshape(hypotheses, local_rows, extent)
    vertical_above = jnp.concatenate([vertical_edge[None], vertical[:-1]], axis=0)
    flux = vertical[None] * slope_y
    flux_above = jnp.concatenate([flux_edge[:, None], flux[:, :-1]], axis=1)
    along = horizontal[None] * slope_x
    loads = weights[None] * targets + jnp.roll(along, 1, axis=2) - along + flux_above - flux
    loads = jnp.transpose(loads, (1, 0, 2))
    diagonal = jnp.roll(horizontal, 1, axis=1) + horizontal + vertical_above + vertical + weights
    blocks = jax.vmap(row_matrix)(diagonal, horizontal)
    zeros_mat = jnp.zeros((extent, extent), jnp.float32)
    zeros_vec = jnp.zeros((hypotheses, extent), jnp.float32)
    identity = jnp.eye(extent, dtype=jnp.float32)
    start = (zeros_mat, -jnp.diag(vertical_above[0]), blocks[0], zeros_vec, loads[0])

    def fold_step(segment, inputs):
        matrix_row, coupling, load_row = inputs
        piece = (zeros_mat, -jnp.diag(coupling), matrix_row, zeros_vec, load_row)
        merged = merge_whole(segment, piece)
        return (merged, None)

    segment, _ = lax.scan(fold_step, start, (blocks[1:], vertical_above[1:], loads[1:]))
    filled = segment + (jnp.zeros((), jnp.float32),)
    blank = (zeros_mat, zeros_mat, identity, zeros_vec, zeros_vec, jnp.ones((), jnp.float32))
    prefix = carried_in(filled, "strip", merge_flagged, blank, False)
    prefix_matrix, prefix_load = (prefix[2], prefix[4])

    def eliminate(state, inputs):
        inverse_prev, load_prev, pivot_prev = state
        matrix_row, coupling, load_row, coupling_below = inputs
        pivot = matrix_row - coupling[:, None] * inverse_prev * coupling[None, :]
        carried = load_row + coupling[None, :] * apply_to(inverse_prev, load_prev)
        inverse_now = inverse(pivot)
        return (
            (inverse_now, carried, pivot),
            (inverse_now * coupling_below[None, :], apply_to(inverse_now, carried)),
        )

    final_state, (gains, offsets) = lax.scan(
        eliminate,
        (inverse(prefix_matrix), prefix_load, identity),
        (blocks, vertical_above, loads, vertical),
    )

    def compose(mapping, inputs):
        gain, offset = inputs
        return ((product(gain, mapping[0]), offset + apply_to(gain, mapping[1])), None)

    (reach, moved), _ = lax.scan(compose, (identity, zeros_vec), (gains, offsets), reverse=True)
    beyond = carried_in((reach, moved), "strip", chain_maps, (identity, zeros_vec), True)
    _, solution = lax.scan(substitute, beyond[1], (gains, offsets), reverse=True)
    solution = jnp.transpose(solution, (1, 0, 2))
    return lax.dynamic_slice_in_dim(solution, lax.axis_index("panel") * slice_cols, slice_cols, 2)


def lane_block(shape, rows):
    return lax.broadcasted_iota(jnp.int32, shape, 1) // rows


def eliminate_column(systems, rows, group):
    row_ids = lax.broadcasted_iota(jnp.int32, systems[0].shape, 0)
    shape = systems[0].shape
    systems = list(systems)
    for first in range(0, rows, group):
        columns = [
            [jnp.broadcast_to(m[:, rows + first + t : rows + first + t + 1], shape) for t in range(group)]
            for m in systems
        ]
        for t in range(group):
            k = first + t
            for b in range(len(systems)):
                column = columns[b][t]
                scale = 1.0 / column[k : k + 1]
                pivot = systems[b][k : k + 1] * scale
                systems[b] = jnp.where(row_ids == k, pivot, systems[b] - column * pivot)
                for u in range(t + 1, group):
                    later = columns[b][u]
                    part = later[k : k + 1] * scale
                    columns[b][u] = jnp.where(row_ids == k, part, later - column * part)
    return systems


def merge_segments(tops, bottoms, rows):
    pairs = len(tops) // 2
    group = max(1, 4 // pairs)
    lanes = tops[0].shape[1]
    block = lane_block(tops[0].shape, rows)
    zero = jnp.zeros((rows, lanes), jnp.float32)
    solved = eliminate_column(
        [bottoms[2 * i] + tops[2 * i + 1] for i in range(pairs)], rows, group
    )
    new_tops, new_bottoms = [], []
    for i, x in enumerate(solved):
        x_top = jnp.where(block == 0, 0.0, jnp.where(block == 1, pltpu.roll(x, rows, 1), x))
        x_bottom = jnp.where(block == 2, 0.0, jnp.where(block == 1, pltpu.roll(x, lanes - rows, 1), x))
        right = jnp.concatenate([x_bottom, zero, x_top, zero], axis=0)
        west, east = tops[2 * i], bottoms[2 * i + 1]
        change = product(jnp.concatenate([west, east], axis=0), right)
        new_tops.append(jnp.where(block == 2, 0.0, west) - change[:rows])
        new_bottoms.append(jnp.where(block == 0, 0.0, east) - change[rows:])
    return solved, new_tops, new_bottoms


def merge_tree(tops, bottoms, rows, kept_ref):
    position = 0
    while len(tops) > 1:
        solved, tops, bottoms = merge_segments(tops, bottoms, rows)
        for x in solved:
            kept_ref[position] = x
            position += 1
    return tops[0], bottoms[0]


def middle(x, west, east, rows):
    zero = jnp.zeros_like(x)
    right = jnp.concatenate([west, zero, east, zero], axis=0)
    return jnp.where(lane_block(x.shape, rows) == 3, x - product(x, right), 0.0)


def descend(kept_ref, leaves, leaf, west, east, rows):
    position, count = leaves - 2, 1
    while count < leaves:
        held = kept_ref[position + (leaf * count) // leaves]
        mid = middle(held, west, east, rows)
        go_east = ((leaf * 2 * count) // leaves) % 2 == 1
        west, east = jnp.where(go_east, mid, west), jnp.where(go_east, east, mid)
        count *= 2
        position -= count
    return west, east


def local_kernel(fields_ref, segment_ref, kept_ref, *, rows, maps):
    count, _, lanes = fields_ref.shape
    shape = (rows, lanes)
    block = lane_block(shape, rows)
    lane = lax.broadcasted_iota(jnp.int32, shape, 1)
    row = lax.broadcasted_iota(jnp.int32, shape, 0)
    diag0, diag1, diag2 = lane == row, lane == row + rows, lane == row + 2 * rows
    upper, lower = lane == row + rows + 1, lane == row + rows - 1
    upper = jnp.logical_and(upper, block == 1)
    lower = jnp.logical_and(lower, block == 1)
    load_lane = jnp.logical_and(lane >= 3 * rows, lane < 3 * rows + maps)
    tops, bottoms = [], []
    for j in range(count):
        f = fields_ref[j]
        above = jnp.where(row == 0, 0.0, pltpu.roll(f, 1, 0))
        h = jnp.broadcast_to(f[:, 0:1], shape)
        v = jnp.broadcast_to(f[:, 1:2], shape)
        w = jnp.broadcast_to(f[:, 2:3], shape)
        va = jnp.broadcast_to(above[:, 1:2], shape)
        flux_above = pltpu.roll(above, 2 * rows, 1)
        along = pltpu.roll(f, rows, 1)
        top = (
            jnp.where(diag1, h + va + v + w, 0.0)
            - jnp.where(upper, v, 0.0)
            - jnp.where(lower, va, 0.0)
            - jnp.where(diag2, h, 0.0)
            + jnp.where(load_lane, f + flux_above, 0.0)
        )
        bottom = jnp.where(diag1, h, 0.0) - jnp.where(diag0, h, 0.0) + jnp.where(load_lane, along, 0.0)
        tops.append(top)
        bottoms.append(bottom)
    top, bottom = merge_tree(tops, bottoms, rows, kept_ref)
    segment_ref[0:rows] = top
    segment_ref[rows : 2 * rows] = bottom


def group_kernel(segments_ref, segment_ref, kept_ref, *, rows):
    count = segments_ref.shape[0]
    tops = [segments_ref[i, 0:rows] for i in range(count)]
    bottoms = [segments_ref[i, rows : 2 * rows] for i in range(count)]
    top, bottom = merge_tree(tops, bottoms, rows, kept_ref)
    segment_ref[0:rows] = top
    segment_ref[rows : 2 * rows] = bottom


def final_kernel(
    where_ref, segments_ref, kept_local_ref, kept_strip_ref, values_ref, kept_panel_ref, *, rows, strips, panels
):
    lanes = segments_ref.shape[2]
    block = lane_block((rows, lanes), rows)
    tops = [segments_ref[i, 0:rows] for i in range(panels)]
    bottoms = [segments_ref[i, rows : 2 * rows] for i in range(panels)]
    top, bottom = merge_tree(tops, bottoms, rows, kept_panel_ref)
    wrap = pltpu.roll(top, lanes - rows, 1) + pltpu.roll(bottom, rows, 1)
    closing = top + bottom + jnp.where(block == 1, wrap, 0.0)
    first = eliminate_column([closing], rows, 4)[0]
    first = jnp.where(block == 3, first, 0.0)
    west, east = descend(kept_panel_ref, panels, where_ref[1], first, first, rows)
    west, east = descend(kept_strip_ref, strips, where_ref[0], west, east, rows)
    count = values_ref.shape[0]
    edges = [west, east]
    position = count - 2
    while len(edges) - 1 < count:
        spans = len(edges) - 1
        mids = [middle(kept_local_ref[position + i], edges[i], edges[i + 1], rows) for i in range(spans)]
        edges = [e for pair in zip(edges, mids) for e in pair] + [edges[-1]]
        position -= 2 * spans
    for i in range(count):
        values_ref[i] = edges[i]


def power_of_two(n):
    return n >= 2 and n & (n - 1) == 0


def longitude_shards(h_cond, v_cond, confidence, teacher, grad_x, grad_y):
    local_rows, slice_cols = h_cond.shape
    maps = teacher.shape[0]
    strips, panels = lax.axis_size("strip"), lax.axis_size("panel")
    rows, lanes, width = local_rows * strips, 4 * local_rows * strips, slice_cols // strips
    along = h_cond[None] * grad_x
    flux = v_cond[None] * grad_y
    load = confidence[None] * teacher - along - flux
    small = jnp.stack([h_cond, v_cond, confidence], axis=0)

    def padded(part):
        return jnp.pad(part, ((0, rows - part.shape[0]), (0, 0), (0, 0)))

    packed = jnp.concatenate([padded(small), padded(flux), padded(along), padded(load)], axis=0)
    packed = jnp.transpose(packed, (2, 1, 0))
    fields = lax.all_to_all(packed, "strip", 0, 1, tiled=True)
    f32 = jnp.float32

    def shape(*dims):
        return jax.ShapeDtypeStruct(dims, f32)

    segment, kept_local = pl.pallas_call(
        functools.partial(local_kernel, rows=rows, maps=maps),
        out_shape=(shape(2 * rows, lanes), shape(width - 1, rows, lanes)),
    )(fields)
    segments = lax.all_gather(segment, "strip")
    segment, kept_strip = pl.pallas_call(
        functools.partial(group_kernel, rows=rows),
        out_shape=(shape(2 * rows, lanes), shape(strips - 1, rows, lanes)),
    )(segments)
    segments = lax.all_gather(segment, "panel")
    position = jnp.stack([lax.axis_index("strip"), lax.axis_index("panel")]).astype(jnp.int32)
    values = pl.pallas_call(
        functools.partial(final_kernel, rows=rows, strips=strips, panels=panels),
        out_shape=shape(width, rows, lanes),
        in_specs=[pl.BlockSpec(memory_space=pltpu.SMEM)] + [pl.BlockSpec(memory_space=pltpu.VMEM)] * 3,
        scratch_shapes=[pltpu.VMEM((panels - 1, rows, lanes), f32)],
    )(position, segments, kept_local, kept_strip)
    values = values[:, :, 3 * rows : 3 * rows + maps]
    values = lax.all_to_all(values, "strip", 1, 0, tiled=True)
    return jnp.transpose(values, (2, 1, 0))


def shards(h_cond, v_cond, confidence, teacher, grad_x, grad_y):
    strips, panels = lax.axis_size("strip"), lax.axis_size("panel")
    rows, cols = h_cond.shape[0] * strips, h_cond.shape[1]
    width = cols // strips
    short = 4 * rows == 128 and 3 <= rows and teacher.shape[0] <= rows
    even = cols % strips == 0 and all(power_of_two(n) for n in (strips, panels, width))
    body = longitude_shards if short and even else latitude_shards
    return body(h_cond, v_cond, confidence, teacher, grad_x, grad_y)


def solution(mesh):
    in_specs = (
        P("strip", "panel"),
        P("strip", "panel"),
        P("strip", "panel"),
        P(None, "strip", "panel"),
        P(None, "strip", "panel"),
        P(None, "strip", "panel"),
    )
    out_specs = P(None, "strip", "panel")
    return jax.shard_map(shards, mesh=mesh, in_specs=in_specs, out_specs=out_specs, check_vma=False)
```

```python
import functools

import jax
import jax.numpy as jnp
from jax import lax
from jax.experimental import pallas as pl
from jax.experimental.pallas import tpu as pltpu
from jax.sharding import PartitionSpec as P

HIGH = lax.Precision.HIGHEST


def shifted(value, axis, by):
    count = lax.axis_size(axis)
    pairs = [(i, i + by) for i in range(count) if 0 <= i + by < count]
    return lax.ppermute(value, axis, pairs)


def carried_in(value, axis, join, neutral, backward):
    count, mine = (lax.axis_size(axis), lax.axis_index(axis))
    pieces = jax.tree.map(lambda part: lax.all_gather(part, axis), value)
    if backward:
        pieces = jax.tree.map(lambda part: part[::-1], pieces)
        mine = count - 1 - mine
    total = jax.tree.map(
        lambda part, zero: jnp.full_like(part, 0) + jnp.asarray(zero, part.dtype), value, neutral
    )

    def turn(position, total):
        longer = join(total, jax.tree.map(lambda part: part[position], pieces))
        return jax.tree.map(lambda new, old: jnp.where(position < mine, new, old), longer, total)

    return lax.fori_loop(0, count - 1, turn, total)


def product(left, right):
    return jnp.dot(left, right, precision=HIGH, preferred_element_type=jnp.float32)


def apply_to(matrix, vectors):
    return product(vectors, matrix.T)


def row_matrix(diag_row, link_row):
    extent = diag_row.shape[0]
    row_ids = lax.broadcasted_iota(jnp.int32, (extent, extent), 0)
    col_ids = lax.broadcasted_iota(jnp.int32, (extent, extent), 1)
    east = col_ids == (row_ids + 1) % extent
    west = row_ids == (col_ids + 1) % extent
    link = jnp.where(east, link_row[:, None], 0.0) + jnp.where(west, link_row[None, :], 0.0)
    return jnp.where(row_ids == col_ids, diag_row[:, None], 0.0) - link


def inverse(matrix):
    factor = jnp.linalg.cholesky(matrix)
    return jax.scipy.linalg.cho_solve((factor, True), jnp.eye(matrix.shape[0], dtype=jnp.float32))


def load_update(factor, upper, lower):
    vector = jax.scipy.linalg.cho_solve((factor, True), (upper[4] + lower[3]).T)
    return (upper[3] - product(upper[1], vector).T, lower[4] - product(lower[1].T, vector).T)


def merge_whole(upper, lower):
    extent = upper[2].shape[0]
    factor = jnp.linalg.cholesky(upper[2] + lower[0])
    solved = jax.scipy.linalg.cho_solve(
        (factor, True), jnp.concatenate([upper[1].T, lower[1]], axis=1)
    )
    first_cols = solved[:, :extent]
    second_cols = solved[:, extent:]
    first_load, second_load = load_update(factor, upper, lower)
    return (
        upper[0] - product(upper[1], first_cols),
        -product(upper[1], second_cols),
        lower[2] - product(lower[1].T, second_cols),
        first_load,
        second_load,
    )


def merge_flagged(upper, lower):
    merged = merge_whole(upper[:5], lower[:5])
    upper_empty = upper[5] > 0.5
    lower_empty = lower[5] > 0.5
    picked = tuple(
        (
            jnp.where(upper_empty, lower_part, jnp.where(lower_empty, upper_part, merged_part))
            for upper_part, lower_part, merged_part in zip(upper[:5], lower[:5], merged)
        )
    )
    return picked + (upper[5] * lower[5],)


def chain_maps(earlier_map, later_map):
    return (
        product(later_map[0], earlier_map[0]),
        later_map[1] + apply_to(later_map[0], earlier_map[1]),
    )


def substitute(value_below, inputs):
    gain, offset = inputs
    value = offset + apply_to(gain, value_below)
    return (value, value)


def latitude_shards(h_cond, v_cond, confidence, teacher, grad_x, grad_y):
    slice_cols = h_cond.shape[1]
    local_rows = h_cond.shape[0]
    hypotheses = teacher.shape[0]
    edge_rows = jnp.concatenate([v_cond[-1][None], v_cond[-1][None] * grad_y[:, -1]], axis=0)
    above = shifted(edge_rows, "strip", 1)
    packed = jnp.concatenate(
        [
            h_cond,
            v_cond,
            confidence,
            above,
            teacher.reshape(hypotheses * local_rows, slice_cols),
            grad_x.reshape(hypotheses * local_rows, slice_cols),
            grad_y.reshape(hypotheses * local_rows, slice_cols),
        ],
        axis=0,
    )
    whole = lax.all_gather(packed, "panel", axis=1, tiled=True)
    extent = whole.shape[1]
    horizontal = whole[:local_rows]
    vertical = whole[local_rows : 2 * local_rows]
    weights = whole[2 * local_rows : 3 * local_rows]
    vertical_edge = whole[3 * local_rows]
    flux_edge = whole[3 * local_rows + 1 : 3 * local_rows + 1 + hypotheses]
    base = 3 * local_rows + 1 + hypotheses
    stride = hypotheses * local_rows
    targets = whole[base : base + stride].reshape(hypotheses, local_rows, extent)
    slope_x = whole[base + stride : base + 2 * stride].reshape(hypotheses, local_rows, extent)
    slope_y = whole[base + 2 * stride : base + 3 * stride].reshape(hypotheses, local_rows, extent)
    vertical_above = jnp.concatenate([vertical_edge[None], vertical[:-1]], axis=0)
    flux = vertical[None] * slope_y
    flux_above = jnp.concatenate([flux_edge[:, None], flux[:, :-1]], axis=1)
    along = horizontal[None] * slope_x
    loads = weights[None] * targets + jnp.roll(along, 1, axis=2) - along + flux_above - flux
    loads = jnp.transpose(loads, (1, 0, 2))
    diagonal = jnp.roll(horizontal, 1, axis=1) + horizontal + vertical_above + vertical + weights
    blocks = jax.vmap(row_matrix)(diagonal, horizontal)
    zeros_mat = jnp.zeros((extent, extent), jnp.float32)
    zeros_vec = jnp.zeros((hypotheses, extent), jnp.float32)
    identity = jnp.eye(extent, dtype=jnp.float32)
    start = (zeros_mat, -jnp.diag(vertical_above[0]), blocks[0], zeros_vec, loads[0])

    def fold_step(segment, inputs):
        matrix_row, coupling, load_row = inputs
        piece = (zeros_mat, -jnp.diag(coupling), matrix_row, zeros_vec, load_row)
        merged = merge_whole(segment, piece)
        return (merged, None)

    segment, _ = lax.scan(fold_step, start, (blocks[1:], vertical_above[1:], loads[1:]))
    filled = segment + (jnp.zeros((), jnp.float32),)
    blank = (zeros_mat, zeros_mat, identity, zeros_vec, zeros_vec, jnp.ones((), jnp.float32))
    prefix = carried_in(filled, "strip", merge_flagged, blank, False)
    prefix_matrix, prefix_load = (prefix[2], prefix[4])

    def eliminate(state, inputs):
        inverse_prev, load_prev, pivot_prev = state
        matrix_row, coupling, load_row, coupling_below = inputs
        pivot = matrix_row - coupling[:, None] * inverse_prev * coupling[None, :]
        carried = load_row + coupling[None, :] * apply_to(inverse_prev, load_prev)
        inverse_now = inverse(pivot)
        return (
            (inverse_now, carried, pivot),
            (inverse_now * coupling_below[None, :], apply_to(inverse_now, carried)),
        )

    final_state, (gains, offsets) = lax.scan(
        eliminate,
        (inverse(prefix_matrix), prefix_load, identity),
        (blocks, vertical_above, loads, vertical),
    )

    def compose(mapping, inputs):
        gain, offset = inputs
        return ((product(gain, mapping[0]), offset + apply_to(gain, mapping[1])), None)

    (reach, moved), _ = lax.scan(compose, (identity, zeros_vec), (gains, offsets), reverse=True)
    beyond = carried_in((reach, moved), "strip", chain_maps, (identity, zeros_vec), True)
    _, solution = lax.scan(substitute, beyond[1], (gains, offsets), reverse=True)
    solution = jnp.transpose(solution, (1, 0, 2))
    return lax.dynamic_slice_in_dim(solution, lax.axis_index("panel") * slice_cols, slice_cols, 2)


def lane_block(shape, rows):
    return lax.broadcasted_iota(jnp.int32, shape, 1) // rows


def eliminate_column(systems, rows, group):
    row_ids = lax.broadcasted_iota(jnp.int32, systems[0].shape, 0)
    shape = systems[0].shape
    systems = list(systems)
    for first in range(0, rows, group):
        columns = [
            [jnp.broadcast_to(m[:, rows + first + t : rows + first + t + 1], shape) for t in range(group)]
            for m in systems
        ]
        for t in range(group):
            k = first + t
            for b in range(len(systems)):
                column = columns[b][t]
                scale = 1.0 / column[k : k + 1]
                pivot = systems[b][k : k + 1] * scale
                systems[b] = jnp.where(row_ids == k, pivot, systems[b] - column * pivot)
                for u in range(t + 1, group):
                    later = columns[b][u]
                    part = later[k : k + 1] * scale
                    columns[b][u] = jnp.where(row_ids == k, part, later - column * part)
    return systems


def merge_segments(tops, bottoms, rows):
    pairs = len(tops) // 2
    group = max(1, 4 // pairs)
    lanes = tops[0].shape[1]
    block = lane_block(tops[0].shape, rows)
    zero = jnp.zeros((rows, lanes), jnp.float32)
    solved = eliminate_column(
        [bottoms[2 * i] + tops[2 * i + 1] for i in range(pairs)], rows, group
    )
    new_tops, new_bottoms = [], []
    for i, x in enumerate(solved):
        x_top = jnp.where(block == 0, 0.0, jnp.where(block == 1, pltpu.roll(x, rows, 1), x))
        x_bottom = jnp.where(block == 2, 0.0, jnp.where(block == 1, pltpu.roll(x, lanes - rows, 1), x))
        right = jnp.concatenate([x_bottom, zero, x_top, zero], axis=0)
        west, east = tops[2 * i], bottoms[2 * i + 1]
        change = product(jnp.concatenate([west, east], axis=0), right)
        new_tops.append(jnp.where(block == 2, 0.0, west) - change[:rows])
        new_bottoms.append(jnp.where(block == 0, 0.0, east) - change[rows:])
    return solved, new_tops, new_bottoms


def merge_tree(tops, bottoms, rows, kept_ref):
    position = 0
    while len(tops) > 1:
        solved, tops, bottoms = merge_segments(tops, bottoms, rows)
        for x in solved:
            kept_ref[position] = x
            position += 1
    return tops[0], bottoms[0]


def middle(x, west, east, rows):
    zero = jnp.zeros_like(x)
    right = jnp.concatenate([west, zero, east, zero], axis=0)
    return jnp.where(lane_block(x.shape, rows) == 3, x - product(x, right), 0.0)


def load_segments(fields_ref, rows, maps):
    count, _, lanes = fields_ref.shape
    shape = (rows, lanes)
    block = lane_block(shape, rows)
    lane = lax.broadcasted_iota(jnp.int32, shape, 1)
    row = lax.broadcasted_iota(jnp.int32, shape, 0)
    diag0, diag1, diag2 = lane == row, lane == row + rows, lane == row + 2 * rows
    upper = jnp.logical_and(lane == row + rows + 1, block == 1)
    lower = jnp.logical_and(lane == row + rows - 1, block == 1)
    load_lane = jnp.logical_and(lane >= 3 * rows, lane < 3 * rows + maps)
    tops, bottoms = [], []
    for j in range(count):
        f = fields_ref[j]
        above = jnp.where(row == 0, 0.0, pltpu.roll(f, 1, 0))
        h = jnp.broadcast_to(f[:, 0:1], shape)
        v = jnp.broadcast_to(f[:, 1:2], shape)
        w = jnp.broadcast_to(f[:, 2:3], shape)
        va = jnp.broadcast_to(above[:, 1:2], shape)
        flux_above = pltpu.roll(above, 2 * rows, 1)
        along = pltpu.roll(f, rows, 1)
        tops.append(
            jnp.where(diag1, h + va + v + w, 0.0)
            - jnp.where(upper, v, 0.0)
            - jnp.where(lower, va, 0.0)
            - jnp.where(diag2, h, 0.0)
            + jnp.where(load_lane, f + flux_above, 0.0)
        )
        bottoms.append(
            jnp.where(diag1, h, 0.0) - jnp.where(diag0, h, 0.0) + jnp.where(load_lane, along, 0.0)
        )
    return tops, bottoms


def partner_of(axis, step):
    me = lax.axis_index(axis)
    side = (me // (1 << step)) % 2
    return me + (1 - 2 * side) * (1 << step), side


def swap_blocks(axis, source_ref, target_ref, send, recv):
    count, me = lax.axis_size(axis), lax.axis_index(axis)
    copies = []
    for step in range(1, count):
        peer = (me + step) % count
        copy = pltpu.make_async_remote_copy(
            src_ref=source_ref.at[peer],
            dst_ref=target_ref.at[me],
            send_sem=send.at[step - 1],
            recv_sem=recv.at[step - 1],
            device_id={axis: peer},
            device_id_type=pl.DeviceIdType.MESH,
        )
        copy.start()
        copies.append(copy)
    target_ref[me] = source_ref[me]
    for copy in copies:
        copy.wait()


def solve_kernel(
    parts_ref, out_ref, got_ref, fields_ref, local_ref, path_ref, mine_ref, theirs_ref, done_ref,
    send_in, recv_in, send_merge, recv_merge, send_out, recv_out, *, rows, maps, strip_steps, panel_steps,
):
    strips, me = lax.axis_size("strip"), lax.axis_index("strip")
    width, _, lanes = fields_ref.shape
    local_rows = rows // strips
    hops = [("strip", s) for s in range(strip_steps)] + [("panel", s) for s in range(panel_steps)]
    barrier = pltpu.get_barrier_semaphore()
    greeted = [("strip", (me + s) % strips) for s in range(1, strips)]
    greeted += [("panel", partner_of("panel", s)[0]) for s in range(panel_steps)]
    for axis, peer in greeted:
        pl.semaphore_signal(barrier, inc=1, device_id={axis: peer}, device_id_type=pl.DeviceIdType.MESH)
    pl.semaphore_wait(barrier, len(greeted))

    swap_blocks("strip", parts_ref, got_ref, send_in, recv_in)
    for s in range(strips):
        for j in range(width):
            fields_ref[j, s * local_rows : (s + 1) * local_rows] = got_ref[
                s, j * local_rows : (j + 1) * local_rows
            ]
    tops, bottoms = load_segments(fields_ref, rows, maps)
    top, bottom = merge_tree(tops, bottoms, rows, local_ref)
    for level, (axis, step) in enumerate(hops):
        partner, side = partner_of(axis, step)
        mine_ref[level, 0:rows] = top
        mine_ref[level, rows : 2 * rows] = bottom
        copy = pltpu.make_async_remote_copy(
            src_ref=mine_ref.at[level],
            dst_ref=theirs_ref.at[level],
            send_sem=send_merge.at[level],
            recv_sem=recv_merge.at[level],
            device_id={axis: partner},
            device_id_type=pl.DeviceIdType.MESH,
        )
        copy.start()
        copy.wait()
        other_top, other_bottom = theirs_ref[level, 0:rows], theirs_ref[level, rows : 2 * rows]
        east = side == 1
        pair_tops = [jnp.where(east, other_top, top), jnp.where(east, top, other_top)]
        pair_bottoms = [jnp.where(east, other_bottom, bottom), jnp.where(east, bottom, other_bottom)]
        solved, new_tops, new_bottoms = merge_segments(pair_tops, pair_bottoms, rows)
        path_ref[level] = solved[0]
        top, bottom = new_tops[0], new_bottoms[0]

    block = lane_block((rows, lanes), rows)
    wrap = pltpu.roll(top, lanes - rows, 1) + pltpu.roll(bottom, rows, 1)
    closing = top + bottom + jnp.where(block == 1, wrap, 0.0)
    first = eliminate_column([closing], rows, 4)[0]
    west = east = jnp.where(block == 3, first, 0.0)
    for level in reversed(range(len(hops))):
        _, side = partner_of(*hops[level])
        mid = middle(path_ref[level], west, east, rows)
        west, east = jnp.where(side == 1, mid, west), jnp.where(side == 1, east, mid)
    edges = [west, east]
    position = width - 2
    while len(edges) - 1 < width:
        spans = len(edges) - 1
        mids = [middle(local_ref[position + i], edges[i], edges[i + 1], rows) for i in range(spans)]
        edges = [e for pair in zip(edges, mids) for e in pair] + [edges[-1]]
        position -= 2 * spans
    for s in range(strips):
        for j in range(width):
            done_ref[s, j * local_rows : (j + 1) * local_rows] = edges[j][
                s * local_rows : (s + 1) * local_rows
            ]
    swap_blocks("strip", done_ref, out_ref, send_out, recv_out)


def power_of_two(n):
    return n >= 2 and n & (n - 1) == 0


def longitude_shards(h_cond, v_cond, confidence, teacher, grad_x, grad_y):
    local_rows, slice_cols = h_cond.shape
    maps = teacher.shape[0]
    strips, panels = lax.axis_size("strip"), lax.axis_size("panel")
    rows, lanes, width = local_rows * strips, 4 * local_rows * strips, slice_cols // strips
    strip_steps, panel_steps = strips.bit_length() - 1, panels.bit_length() - 1
    levels = strip_steps + panel_steps
    along = h_cond[None] * grad_x
    flux = v_cond[None] * grad_y
    load = confidence[None] * teacher - along - flux
    small = jnp.stack([h_cond, v_cond, confidence], axis=0)

    def padded(part):
        return jnp.pad(part, ((0, rows - part.shape[0]), (0, 0), (0, 0)))

    packed = jnp.concatenate([padded(small), padded(flux), padded(along), padded(load)], axis=0)
    packed = jnp.transpose(packed, (2, 1, 0)).reshape(strips, width * local_rows, lanes)
    f32 = jnp.float32
    dma = pltpu.SemaphoreType.DMA
    values = pl.pallas_call(
        functools.partial(
            solve_kernel, rows=rows, maps=maps, strip_steps=strip_steps, panel_steps=panel_steps
        ),
        out_shape=jax.ShapeDtypeStruct((strips, width * local_rows, lanes), f32),
        in_specs=[pl.BlockSpec(memory_space=pltpu.VMEM)],
        out_specs=pl.BlockSpec(memory_space=pltpu.VMEM),
        scratch_shapes=[
            pltpu.VMEM((strips, width * local_rows, lanes), f32),
            pltpu.VMEM((width, rows, lanes), f32),
            pltpu.VMEM((width - 1, rows, lanes), f32),
            pltpu.VMEM((levels, rows, lanes), f32),
            pltpu.VMEM((levels, 2 * rows, lanes), f32),
            pltpu.VMEM((levels, 2 * rows, lanes), f32),
            pltpu.VMEM((strips, width * local_rows, lanes), f32),
            dma((strips - 1,)),
            dma((strips - 1,)),
            dma((levels,)),
            dma((levels,)),
            dma((strips - 1,)),
            dma((strips - 1,)),
        ],
        compiler_params=pltpu.CompilerParams(collective_id=0, has_side_effects=True),
    )(packed)
    values = values.reshape(slice_cols, local_rows, lanes)[:, :, 3 * rows : 3 * rows + maps]
    return jnp.transpose(values, (2, 1, 0))


def shards(h_cond, v_cond, confidence, teacher, grad_x, grad_y):
    strips, panels = lax.axis_size("strip"), lax.axis_size("panel")
    rows, cols = h_cond.shape[0] * strips, h_cond.shape[1]
    width = cols // strips
    short = 4 * rows == 128 and 3 <= rows and teacher.shape[0] <= rows
    even = cols % strips == 0 and all(power_of_two(n) for n in (strips, panels, width))
    body = longitude_shards if short and even else latitude_shards
    return body(h_cond, v_cond, confidence, teacher, grad_x, grad_y)


def solution(mesh):
    in_specs = (
        P("strip", "panel"),
        P("strip", "panel"),
        P("strip", "panel"),
        P(None, "strip", "panel"),
        P(None, "strip", "panel"),
        P(None, "strip", "panel"),
    )
    out_specs = P(None, "strip", "panel")
    return jax.shard_map(shards, mesh=mesh, in_specs=in_specs, out_specs=out_specs, check_vma=False)
```

```python
import functools

import jax
import jax.numpy as jnp
from jax import lax
from jax.experimental import pallas as pl
from jax.experimental.pallas import tpu as pltpu
from jax.sharding import PartitionSpec as P

HIGH = lax.Precision.HIGHEST


def shifted(value, axis, by):
    count = lax.axis_size(axis)
    pairs = [(i, i + by) for i in range(count) if 0 <= i + by < count]
    return lax.ppermute(value, axis, pairs)


def carried_in(value, axis, join, neutral, backward):
    count, mine = (lax.axis_size(axis), lax.axis_index(axis))
    pieces = jax.tree.map(lambda part: lax.all_gather(part, axis), value)
    if backward:
        pieces = jax.tree.map(lambda part: part[::-1], pieces)
        mine = count - 1 - mine
    total = jax.tree.map(
        lambda part, zero: jnp.full_like(part, 0) + jnp.asarray(zero, part.dtype), value, neutral
    )

    def turn(position, total):
        longer = join(total, jax.tree.map(lambda part: part[position], pieces))
        return jax.tree.map(lambda new, old: jnp.where(position < mine, new, old), longer, total)

    return lax.fori_loop(0, count - 1, turn, total)


def product(left, right):
    return jnp.dot(left, right, precision=HIGH, preferred_element_type=jnp.float32)


def apply_to(matrix, vectors):
    return product(vectors, matrix.T)


def row_matrix(diag_row, link_row):
    extent = diag_row.shape[0]
    row_ids = lax.broadcasted_iota(jnp.int32, (extent, extent), 0)
    col_ids = lax.broadcasted_iota(jnp.int32, (extent, extent), 1)
    east = col_ids == (row_ids + 1) % extent
    west = row_ids == (col_ids + 1) % extent
    link = jnp.where(east, link_row[:, None], 0.0) + jnp.where(west, link_row[None, :], 0.0)
    return jnp.where(row_ids == col_ids, diag_row[:, None], 0.0) - link


def inverse(matrix):
    factor = jnp.linalg.cholesky(matrix)
    return jax.scipy.linalg.cho_solve((factor, True), jnp.eye(matrix.shape[0], dtype=jnp.float32))


def load_update(factor, upper, lower):
    vector = jax.scipy.linalg.cho_solve((factor, True), (upper[4] + lower[3]).T)
    return (upper[3] - product(upper[1], vector).T, lower[4] - product(lower[1].T, vector).T)


def merge_whole(upper, lower):
    extent = upper[2].shape[0]
    factor = jnp.linalg.cholesky(upper[2] + lower[0])
    solved = jax.scipy.linalg.cho_solve(
        (factor, True), jnp.concatenate([upper[1].T, lower[1]], axis=1)
    )
    first_cols = solved[:, :extent]
    second_cols = solved[:, extent:]
    first_load, second_load = load_update(factor, upper, lower)
    return (
        upper[0] - product(upper[1], first_cols),
        -product(upper[1], second_cols),
        lower[2] - product(lower[1].T, second_cols),
        first_load,
        second_load,
    )


def merge_flagged(upper, lower):
    merged = merge_whole(upper[:5], lower[:5])
    upper_empty = upper[5] > 0.5
    lower_empty = lower[5] > 0.5
    picked = tuple(
        (
            jnp.where(upper_empty, lower_part, jnp.where(lower_empty, upper_part, merged_part))
            for upper_part, lower_part, merged_part in zip(upper[:5], lower[:5], merged)
        )
    )
    return picked + (upper[5] * lower[5],)


def chain_maps(earlier_map, later_map):
    return (
        product(later_map[0], earlier_map[0]),
        later_map[1] + apply_to(later_map[0], earlier_map[1]),
    )


def substitute(value_below, inputs):
    gain, offset = inputs
    value = offset + apply_to(gain, value_below)
    return (value, value)


def latitude_shards(h_cond, v_cond, confidence, teacher, grad_x, grad_y):
    slice_cols = h_cond.shape[1]
    local_rows = h_cond.shape[0]
    hypotheses = teacher.shape[0]
    edge_rows = jnp.concatenate([v_cond[-1][None], v_cond[-1][None] * grad_y[:, -1]], axis=0)
    above = shifted(edge_rows, "strip", 1)
    packed = jnp.concatenate(
        [
            h_cond,
            v_cond,
            confidence,
            above,
            teacher.reshape(hypotheses * local_rows, slice_cols),
            grad_x.reshape(hypotheses * local_rows, slice_cols),
            grad_y.reshape(hypotheses * local_rows, slice_cols),
        ],
        axis=0,
    )
    whole = lax.all_gather(packed, "panel", axis=1, tiled=True)
    extent = whole.shape[1]
    horizontal = whole[:local_rows]
    vertical = whole[local_rows : 2 * local_rows]
    weights = whole[2 * local_rows : 3 * local_rows]
    vertical_edge = whole[3 * local_rows]
    flux_edge = whole[3 * local_rows + 1 : 3 * local_rows + 1 + hypotheses]
    base = 3 * local_rows + 1 + hypotheses
    stride = hypotheses * local_rows
    targets = whole[base : base + stride].reshape(hypotheses, local_rows, extent)
    slope_x = whole[base + stride : base + 2 * stride].reshape(hypotheses, local_rows, extent)
    slope_y = whole[base + 2 * stride : base + 3 * stride].reshape(hypotheses, local_rows, extent)
    vertical_above = jnp.concatenate([vertical_edge[None], vertical[:-1]], axis=0)
    flux = vertical[None] * slope_y
    flux_above = jnp.concatenate([flux_edge[:, None], flux[:, :-1]], axis=1)
    along = horizontal[None] * slope_x
    loads = weights[None] * targets + jnp.roll(along, 1, axis=2) - along + flux_above - flux
    loads = jnp.transpose(loads, (1, 0, 2))
    diagonal = jnp.roll(horizontal, 1, axis=1) + horizontal + vertical_above + vertical + weights
    blocks = jax.vmap(row_matrix)(diagonal, horizontal)
    zeros_mat = jnp.zeros((extent, extent), jnp.float32)
    zeros_vec = jnp.zeros((hypotheses, extent), jnp.float32)
    identity = jnp.eye(extent, dtype=jnp.float32)
    start = (zeros_mat, -jnp.diag(vertical_above[0]), blocks[0], zeros_vec, loads[0])

    def fold_step(segment, inputs):
        matrix_row, coupling, load_row = inputs
        piece = (zeros_mat, -jnp.diag(coupling), matrix_row, zeros_vec, load_row)
        merged = merge_whole(segment, piece)
        return (merged, None)

    segment, _ = lax.scan(fold_step, start, (blocks[1:], vertical_above[1:], loads[1:]))
    filled = segment + (jnp.zeros((), jnp.float32),)
    blank = (zeros_mat, zeros_mat, identity, zeros_vec, zeros_vec, jnp.ones((), jnp.float32))
    prefix = carried_in(filled, "strip", merge_flagged, blank, False)
    prefix_matrix, prefix_load = (prefix[2], prefix[4])

    def eliminate(state, inputs):
        inverse_prev, load_prev, pivot_prev = state
        matrix_row, coupling, load_row, coupling_below = inputs
        pivot = matrix_row - coupling[:, None] * inverse_prev * coupling[None, :]
        carried = load_row + coupling[None, :] * apply_to(inverse_prev, load_prev)
        inverse_now = inverse(pivot)
        return (
            (inverse_now, carried, pivot),
            (inverse_now * coupling_below[None, :], apply_to(inverse_now, carried)),
        )

    final_state, (gains, offsets) = lax.scan(
        eliminate,
        (inverse(prefix_matrix), prefix_load, identity),
        (blocks, vertical_above, loads, vertical),
    )

    def compose(mapping, inputs):
        gain, offset = inputs
        return ((product(gain, mapping[0]), offset + apply_to(gain, mapping[1])), None)

    (reach, moved), _ = lax.scan(compose, (identity, zeros_vec), (gains, offsets), reverse=True)
    beyond = carried_in((reach, moved), "strip", chain_maps, (identity, zeros_vec), True)
    _, solution = lax.scan(substitute, beyond[1], (gains, offsets), reverse=True)
    solution = jnp.transpose(solution, (1, 0, 2))
    return lax.dynamic_slice_in_dim(solution, lax.axis_index("panel") * slice_cols, slice_cols, 2)


def lane_block(shape, rows):
    return lax.broadcasted_iota(jnp.int32, shape, 1) // rows


def eliminate_column(systems, rows, group):
    row_ids = lax.broadcasted_iota(jnp.int32, systems[0].shape, 0)
    shape = systems[0].shape
    systems = list(systems)
    for first in range(0, rows, group):
        columns = [
            [jnp.broadcast_to(m[:, rows + first + t : rows + first + t + 1], shape) for t in range(group)]
            for m in systems
        ]
        for t in range(group):
            k = first + t
            for b in range(len(systems)):
                column = columns[b][t]
                scale = 1.0 / column[k : k + 1]
                pivot = systems[b][k : k + 1] * scale
                systems[b] = jnp.where(row_ids == k, pivot, systems[b] - column * pivot)
                for u in range(t + 1, group):
                    later = columns[b][u]
                    part = later[k : k + 1] * scale
                    columns[b][u] = jnp.where(row_ids == k, part, later - column * part)
    return systems


def merge_segments(tops, bottoms, rows):
    pairs = len(tops) // 2
    group = rows // 2 if pairs == 1 else rows // 4
    solved = eliminate_column(
        [bottoms[2 * i] + tops[2 * i + 1] for i in range(pairs)], rows, group
    )
    new_tops, new_bottoms = reduce_segments(solved, tops[::2], bottoms[1::2], rows)
    return solved, new_tops, new_bottoms


def reduce_segments(solved, wests, easts, rows):
    lanes = solved[0].shape[1]
    block = lane_block(solved[0].shape, rows)
    zero = jnp.zeros((rows, lanes), jnp.float32)
    new_tops, new_bottoms = [], []
    for x, west, east in zip(solved, wests, easts):
        x_top = jnp.where(block == 0, 0.0, jnp.where(block == 1, pltpu.roll(x, rows, 1), x))
        x_bottom = jnp.where(block == 2, 0.0, jnp.where(block == 1, pltpu.roll(x, lanes - rows, 1), x))
        right = jnp.concatenate([x_bottom, zero, x_top, zero], axis=0)
        change = product(jnp.concatenate([west, east], axis=0), right)
        new_tops.append(jnp.where(block == 2, 0.0, west) - change[:rows])
        new_bottoms.append(jnp.where(block == 0, 0.0, east) - change[rows:])
    return new_tops, new_bottoms


def merge_tree(tops, bottoms, rows, kept_ref):
    position = 0
    while len(tops) > 1:
        solved, tops, bottoms = merge_segments(tops, bottoms, rows)
        for x in solved:
            kept_ref[position] = x
            position += 1
    return tops[0], bottoms[0]


def middle(x, west, east, rows):
    zero = jnp.zeros_like(x)
    right = jnp.concatenate([west, zero, east, zero], axis=0)
    return jnp.where(lane_block(x.shape, rows) == 3, x - product(x, right), 0.0)


def load_segments(fields_ref, rows, maps):
    count, _, lanes = fields_ref.shape
    shape = (rows, lanes)
    block = lane_block(shape, rows)
    lane = lax.broadcasted_iota(jnp.int32, shape, 1)
    row = lax.broadcasted_iota(jnp.int32, shape, 0)
    diag0, diag1, diag2 = lane == row, lane == row + rows, lane == row + 2 * rows
    upper = jnp.logical_and(lane == row + rows + 1, block == 1)
    lower = jnp.logical_and(lane == row + rows - 1, block == 1)
    load_lane = jnp.logical_and(lane >= 3 * rows, lane < 3 * rows + maps)
    tops, bottoms = [], []
    for j in range(count):
        f = fields_ref[j]
        above = jnp.where(row == 0, 0.0, pltpu.roll(f, 1, 0))
        h = jnp.broadcast_to(f[:, 0:1], shape)
        v = jnp.broadcast_to(f[:, 1:2], shape)
        w = jnp.broadcast_to(f[:, 2:3], shape)
        va = jnp.broadcast_to(above[:, 1:2], shape)
        flux_above = pltpu.roll(above, 2 * rows, 1)
        along = pltpu.roll(f, rows, 1)
        tops.append(
            jnp.where(diag1, h + va + v + w, 0.0)
            - jnp.where(upper, v, 0.0)
            - jnp.where(lower, va, 0.0)
            - jnp.where(diag2, h, 0.0)
            + jnp.where(load_lane, f + flux_above, 0.0)
        )
        bottoms.append(
            jnp.where(diag1, h, 0.0) - jnp.where(diag0, h, 0.0) + jnp.where(load_lane, along, 0.0)
        )
    return tops, bottoms


def partner_of(axis, step):
    me = lax.axis_index(axis)
    side = (me // (1 << step)) % 2
    return me + (1 - 2 * side) * (1 << step), side


def swap_blocks(axis, source_ref, target_ref, send, recv):
    count, me = lax.axis_size(axis), lax.axis_index(axis)
    copies = []
    for step in range(1, count):
        peer = (me + step) % count
        copy = pltpu.make_async_remote_copy(
            src_ref=source_ref.at[peer],
            dst_ref=target_ref.at[me],
            send_sem=send.at[step - 1],
            recv_sem=recv.at[step - 1],
            device_id={axis: peer},
            device_id_type=pl.DeviceIdType.MESH,
        )
        copy.start()
        copies.append(copy)
    target_ref[me] = source_ref[me]
    for copy in copies:
        copy.wait()


def solve_kernel(
    parts_ref, out_ref, got_ref, fields_ref, local_ref, path_ref, mine_ref, theirs_ref, done_ref,
    send_in, recv_in, send_merge, recv_merge, send_out, recv_out, *, rows, maps, strip_steps, panel_steps,
):
    strips, me = lax.axis_size("strip"), lax.axis_index("strip")
    width, _, lanes = fields_ref.shape
    local_rows = rows // strips
    hops = [("strip", s) for s in range(strip_steps)] + [("panel", s) for s in range(panel_steps)]
    barrier = pltpu.get_barrier_semaphore()
    greeted = [("strip", (me + s) % strips) for s in range(1, strips)]
    greeted += [("panel", partner_of("panel", s)[0]) for s in range(panel_steps)]
    for axis, peer in greeted:
        pl.semaphore_signal(barrier, inc=1, device_id={axis: peer}, device_id_type=pl.DeviceIdType.MESH)
    pl.semaphore_wait(barrier, len(greeted))

    swap_blocks("strip", parts_ref, got_ref, send_in, recv_in)
    for s in range(strips):
        for j in range(width):
            fields_ref[j, s * local_rows : (s + 1) * local_rows] = got_ref[
                s, j * local_rows : (j + 1) * local_rows
            ]
    tops, bottoms = load_segments(fields_ref, rows, maps)
    top, bottom = merge_tree(tops, bottoms, rows, local_ref)
    for level, (axis, step) in enumerate(hops):
        partner, side = partner_of(axis, step)
        mine_ref[level, 0] = top
        mine_ref[level, 1] = bottom
        copies = []
        for order, half in enumerate((1 - side, side)):
            copy = pltpu.make_async_remote_copy(
                src_ref=mine_ref.at[level, half],
                dst_ref=theirs_ref.at[level, half],
                send_sem=send_merge.at[level, order],
                recv_sem=recv_merge.at[level, order],
                device_id={axis: partner},
                device_id_type=pl.DeviceIdType.MESH,
            )
            copy.start()
            copies.append(copy)
        east = side == 1
        copies[0].wait()
        facing = jnp.where(east, top, bottom) + theirs_ref[level, side]
        solved = eliminate_column([facing], rows, rows // 2)
        path_ref[level] = solved[0]
        copies[1].wait()
        far = theirs_ref[level, 1 - side]
        new_tops, new_bottoms = reduce_segments(
            solved, [jnp.where(east, far, top)], [jnp.where(east, bottom, far)], rows
        )
        top, bottom = new_tops[0], new_bottoms[0]

    block = lane_block((rows, lanes), rows)
    wrap = pltpu.roll(top, lanes - rows, 1) + pltpu.roll(bottom, rows, 1)
    closing = top + bottom + jnp.where(block == 1, wrap, 0.0)
    first = eliminate_column([closing], rows, rows // 2)[0]
    west = east = jnp.where(block == 3, first, 0.0)
    for level in reversed(range(len(hops))):
        _, side = partner_of(*hops[level])
        mid = middle(path_ref[level], west, east, rows)
        west, east = jnp.where(side == 1, mid, west), jnp.where(side == 1, east, mid)
    edges = [west, east]
    position = width - 2
    while len(edges) - 1 < width:
        spans = len(edges) - 1
        mids = [middle(local_ref[position + i], edges[i], edges[i + 1], rows) for i in range(spans)]
        edges = [e for pair in zip(edges, mids) for e in pair] + [edges[-1]]
        position -= 2 * spans
    slot = lax.broadcasted_iota(jnp.int32, (rows, lanes), 1) // maps
    packed = jnp.zeros((rows, lanes), jnp.float32)
    for j in range(width):
        moved = pltpu.roll(edges[j], (j * maps + rows) % lanes, 1)
        packed = jnp.where(slot == j, moved, packed)
    for s in range(strips):
        done_ref[s] = packed[s * local_rows : (s + 1) * local_rows]
    swap_blocks("strip", done_ref, out_ref, send_out, recv_out)


def power_of_two(n):
    return n >= 2 and n & (n - 1) == 0


def longitude_shards(h_cond, v_cond, confidence, teacher, grad_x, grad_y):
    local_rows, slice_cols = h_cond.shape
    maps = teacher.shape[0]
    strips, panels = lax.axis_size("strip"), lax.axis_size("panel")
    rows, lanes, width = local_rows * strips, 4 * local_rows * strips, slice_cols // strips
    strip_steps, panel_steps = strips.bit_length() - 1, panels.bit_length() - 1
    levels = strip_steps + panel_steps
    along = h_cond[None] * grad_x
    flux = v_cond[None] * grad_y
    load = confidence[None] * teacher - along - flux
    small = jnp.stack([h_cond, v_cond, confidence], axis=0)

    def padded(part):
        return jnp.pad(part, ((0, rows - part.shape[0]), (0, 0), (0, 0)))

    packed = jnp.concatenate([padded(small), padded(flux), padded(along), padded(load)], axis=0)
    packed = jnp.transpose(packed, (2, 1, 0)).reshape(strips, width * local_rows, lanes)
    f32 = jnp.float32
    dma = pltpu.SemaphoreType.DMA
    values = pl.pallas_call(
        functools.partial(
            solve_kernel, rows=rows, maps=maps, strip_steps=strip_steps, panel_steps=panel_steps
        ),
        out_shape=jax.ShapeDtypeStruct((strips, local_rows, lanes), f32),
        in_specs=[pl.BlockSpec(memory_space=pltpu.VMEM)],
        out_specs=pl.BlockSpec(memory_space=pltpu.VMEM),
        scratch_shapes=[
            pltpu.VMEM((strips, width * local_rows, lanes), f32),
            pltpu.VMEM((width, rows, lanes), f32),
            pltpu.VMEM((width - 1, rows, lanes), f32),
            pltpu.VMEM((levels, rows, lanes), f32),
            pltpu.VMEM((levels, 2, rows, lanes), f32),
            pltpu.VMEM((levels, 2, rows, lanes), f32),
            pltpu.VMEM((strips, local_rows, lanes), f32),
            dma((strips - 1,)),
            dma((strips - 1,)),
            dma((levels, 2)),
            dma((levels, 2)),
            dma((strips - 1,)),
            dma((strips - 1,)),
        ],
        compiler_params=pltpu.CompilerParams(collective_id=0, has_side_effects=True),
    )(packed)
    values = values[:, :, : width * maps].reshape(strips, local_rows, width, maps)
    return jnp.transpose(values, (3, 1, 0, 2)).reshape(maps, local_rows, slice_cols)


def shards(h_cond, v_cond, confidence, teacher, grad_x, grad_y):
    strips, panels = lax.axis_size("strip"), lax.axis_size("panel")
    rows, cols = h_cond.shape[0] * strips, h_cond.shape[1]
    width = cols // strips
    short = 4 * rows == 128 and 3 <= rows and teacher.shape[0] <= rows and width * teacher.shape[0] <= 4 * rows
    even = cols % strips == 0 and all(power_of_two(n) for n in (strips, panels, width))
    body = longitude_shards if short and even else latitude_shards
    return body(h_cond, v_cond, confidence, teacher, grad_x, grad_y)


def solution(mesh):
    in_specs = (
        P("strip", "panel"),
        P("strip", "panel"),
        P("strip", "panel"),
        P(None, "strip", "panel"),
        P(None, "strip", "panel"),
        P(None, "strip", "panel"),
    )
    out_specs = P(None, "strip", "panel")
    return jax.shard_map(shards, mesh=mesh, in_specs=in_specs, out_specs=out_specs, check_vma=False)
```

```python
import functools

import jax
import jax.numpy as jnp
from jax import lax
from jax.experimental import pallas as pl
from jax.experimental.pallas import tpu as pltpu
from jax.sharding import PartitionSpec as P

HIGH = lax.Precision.HIGHEST


def shifted(value, axis, by):
    count = lax.axis_size(axis)
    pairs = [(i, i + by) for i in range(count) if 0 <= i + by < count]
    return lax.ppermute(value, axis, pairs)


def carried_in(value, axis, join, neutral, backward):
    count, mine = (lax.axis_size(axis), lax.axis_index(axis))
    pieces = jax.tree.map(lambda part: lax.all_gather(part, axis), value)
    if backward:
        pieces = jax.tree.map(lambda part: part[::-1], pieces)
        mine = count - 1 - mine
    total = jax.tree.map(
        lambda part, zero: jnp.full_like(part, 0) + jnp.asarray(zero, part.dtype), value, neutral
    )

    def turn(position, total):
        longer = join(total, jax.tree.map(lambda part: part[position], pieces))
        return jax.tree.map(lambda new, old: jnp.where(position < mine, new, old), longer, total)

    return lax.fori_loop(0, count - 1, turn, total)


def product(left, right):
    return jnp.dot(left, right, precision=HIGH, preferred_element_type=jnp.float32)


def apply_to(matrix, vectors):
    return product(vectors, matrix.T)


def row_matrix(diag_row, link_row):
    extent = diag_row.shape[0]
    row_ids = lax.broadcasted_iota(jnp.int32, (extent, extent), 0)
    col_ids = lax.broadcasted_iota(jnp.int32, (extent, extent), 1)
    east = col_ids == (row_ids + 1) % extent
    west = row_ids == (col_ids + 1) % extent
    link = jnp.where(east, link_row[:, None], 0.0) + jnp.where(west, link_row[None, :], 0.0)
    return jnp.where(row_ids == col_ids, diag_row[:, None], 0.0) - link


def inverse(matrix):
    factor = jnp.linalg.cholesky(matrix)
    return jax.scipy.linalg.cho_solve((factor, True), jnp.eye(matrix.shape[0], dtype=jnp.float32))


def load_update(factor, upper, lower):
    vector = jax.scipy.linalg.cho_solve((factor, True), (upper[4] + lower[3]).T)
    return (upper[3] - product(upper[1], vector).T, lower[4] - product(lower[1].T, vector).T)


def merge_whole(upper, lower):
    extent = upper[2].shape[0]
    factor = jnp.linalg.cholesky(upper[2] + lower[0])
    solved = jax.scipy.linalg.cho_solve(
        (factor, True), jnp.concatenate([upper[1].T, lower[1]], axis=1)
    )
    first_cols = solved[:, :extent]
    second_cols = solved[:, extent:]
    first_load, second_load = load_update(factor, upper, lower)
    return (
        upper[0] - product(upper[1], first_cols),
        -product(upper[1], second_cols),
        lower[2] - product(lower[1].T, second_cols),
        first_load,
        second_load,
    )


def merge_flagged(upper, lower):
    merged = merge_whole(upper[:5], lower[:5])
    upper_empty = upper[5] > 0.5
    lower_empty = lower[5] > 0.5
    picked = tuple(
        (
            jnp.where(upper_empty, lower_part, jnp.where(lower_empty, upper_part, merged_part))
            for upper_part, lower_part, merged_part in zip(upper[:5], lower[:5], merged)
        )
    )
    return picked + (upper[5] * lower[5],)


def chain_maps(earlier_map, later_map):
    return (
        product(later_map[0], earlier_map[0]),
        later_map[1] + apply_to(later_map[0], earlier_map[1]),
    )


def substitute(value_below, inputs):
    gain, offset = inputs
    value = offset + apply_to(gain, value_below)
    return (value, value)


def latitude_shards(h_cond, v_cond, confidence, teacher, grad_x, grad_y):
    slice_cols = h_cond.shape[1]
    local_rows = h_cond.shape[0]
    hypotheses = teacher.shape[0]
    edge_rows = jnp.concatenate([v_cond[-1][None], v_cond[-1][None] * grad_y[:, -1]], axis=0)
    above = shifted(edge_rows, "strip", 1)
    packed = jnp.concatenate(
        [
            h_cond,
            v_cond,
            confidence,
            above,
            teacher.reshape(hypotheses * local_rows, slice_cols),
            grad_x.reshape(hypotheses * local_rows, slice_cols),
            grad_y.reshape(hypotheses * local_rows, slice_cols),
        ],
        axis=0,
    )
    whole = lax.all_gather(packed, "panel", axis=1, tiled=True)
    extent = whole.shape[1]
    horizontal = whole[:local_rows]
    vertical = whole[local_rows : 2 * local_rows]
    weights = whole[2 * local_rows : 3 * local_rows]
    vertical_edge = whole[3 * local_rows]
    flux_edge = whole[3 * local_rows + 1 : 3 * local_rows + 1 + hypotheses]
    base = 3 * local_rows + 1 + hypotheses
    stride = hypotheses * local_rows
    targets = whole[base : base + stride].reshape(hypotheses, local_rows, extent)
    slope_x = whole[base + stride : base + 2 * stride].reshape(hypotheses, local_rows, extent)
    slope_y = whole[base + 2 * stride : base + 3 * stride].reshape(hypotheses, local_rows, extent)
    vertical_above = jnp.concatenate([vertical_edge[None], vertical[:-1]], axis=0)
    flux = vertical[None] * slope_y
    flux_above = jnp.concatenate([flux_edge[:, None], flux[:, :-1]], axis=1)
    along = horizontal[None] * slope_x
    loads = weights[None] * targets + jnp.roll(along, 1, axis=2) - along + flux_above - flux
    loads = jnp.transpose(loads, (1, 0, 2))
    diagonal = jnp.roll(horizontal, 1, axis=1) + horizontal + vertical_above + vertical + weights
    blocks = jax.vmap(row_matrix)(diagonal, horizontal)
    zeros_mat = jnp.zeros((extent, extent), jnp.float32)
    zeros_vec = jnp.zeros((hypotheses, extent), jnp.float32)
    identity = jnp.eye(extent, dtype=jnp.float32)
    start = (zeros_mat, -jnp.diag(vertical_above[0]), blocks[0], zeros_vec, loads[0])

    def fold_step(segment, inputs):
        matrix_row, coupling, load_row = inputs
        piece = (zeros_mat, -jnp.diag(coupling), matrix_row, zeros_vec, load_row)
        merged = merge_whole(segment, piece)
        return (merged, None)

    segment, _ = lax.scan(fold_step, start, (blocks[1:], vertical_above[1:], loads[1:]))
    filled = segment + (jnp.zeros((), jnp.float32),)
    blank = (zeros_mat, zeros_mat, identity, zeros_vec, zeros_vec, jnp.ones((), jnp.float32))
    prefix = carried_in(filled, "strip", merge_flagged, blank, False)
    prefix_matrix, prefix_load = (prefix[2], prefix[4])

    def eliminate(state, inputs):
        inverse_prev, load_prev, pivot_prev = state
        matrix_row, coupling, load_row, coupling_below = inputs
        pivot = matrix_row - coupling[:, None] * inverse_prev * coupling[None, :]
        carried = load_row + coupling[None, :] * apply_to(inverse_prev, load_prev)
        inverse_now = inverse(pivot)
        return (
            (inverse_now, carried, pivot),
            (inverse_now * coupling_below[None, :], apply_to(inverse_now, carried)),
        )

    final_state, (gains, offsets) = lax.scan(
        eliminate,
        (inverse(prefix_matrix), prefix_load, identity),
        (blocks, vertical_above, loads, vertical),
    )

    def compose(mapping, inputs):
        gain, offset = inputs
        return ((product(gain, mapping[0]), offset + apply_to(gain, mapping[1])), None)

    (reach, moved), _ = lax.scan(compose, (identity, zeros_vec), (gains, offsets), reverse=True)
    beyond = carried_in((reach, moved), "strip", chain_maps, (identity, zeros_vec), True)
    _, solution = lax.scan(substitute, beyond[1], (gains, offsets), reverse=True)
    solution = jnp.transpose(solution, (1, 0, 2))
    return lax.dynamic_slice_in_dim(solution, lax.axis_index("panel") * slice_cols, slice_cols, 2)


def lane_block(shape, rows):
    return lax.broadcasted_iota(jnp.int32, shape, 1) // rows


def eliminate_column(systems, rows, group):
    row_ids = lax.broadcasted_iota(jnp.int32, systems[0].shape, 0)
    shape = systems[0].shape
    systems = list(systems)
    for first in range(0, rows, group):
        columns = [
            [jnp.broadcast_to(m[:, rows + first + t : rows + first + t + 1], shape) for t in range(group)]
            for m in systems
        ]
        for t in range(group):
            k = first + t
            for b in range(len(systems)):
                column = columns[b][t]
                scale = 1.0 / column[k : k + 1]
                pivot = systems[b][k : k + 1] * scale
                systems[b] = jnp.where(row_ids == k, pivot, systems[b] - column * pivot)
                for u in range(t + 1, group):
                    later = columns[b][u]
                    part = later[k : k + 1] * scale
                    columns[b][u] = jnp.where(row_ids == k, part, later - column * part)
    return systems


def merge_segments(tops, bottoms, rows):
    pairs = len(tops) // 2
    group = rows // 2 if pairs == 1 else rows // 4
    solved = eliminate_column(
        [bottoms[2 * i] + tops[2 * i + 1] for i in range(pairs)], rows, group
    )
    new_tops, new_bottoms = reduce_segments(solved, tops[::2], bottoms[1::2], rows)
    return solved, new_tops, new_bottoms


def reduce_segments(solved, wests, easts, rows):
    lanes = solved[0].shape[1]
    block = lane_block(solved[0].shape, rows)
    zero = jnp.zeros((rows, lanes), jnp.float32)
    new_tops, new_bottoms = [], []
    for x, west, east in zip(solved, wests, easts):
        x_top = jnp.where(block == 0, 0.0, jnp.where(block == 1, pltpu.roll(x, rows, 1), x))
        x_bottom = jnp.where(block == 2, 0.0, jnp.where(block == 1, pltpu.roll(x, lanes - rows, 1), x))
        right = jnp.concatenate([x_bottom, zero, x_top, zero], axis=0)
        change = product(jnp.concatenate([west, east], axis=0), right)
        new_tops.append(jnp.where(block == 2, 0.0, west) - change[:rows])
        new_bottoms.append(jnp.where(block == 0, 0.0, east) - change[rows:])
    return new_tops, new_bottoms


def merge_tree(tops, bottoms, rows, kept_ref):
    position = 0
    while len(tops) > 1:
        solved, tops, bottoms = merge_segments(tops, bottoms, rows)
        for x in solved:
            kept_ref[position] = x
            position += 1
    return tops[0], bottoms[0]


def load_segments(fields_ref, rows, maps):
    count, _, lanes = fields_ref.shape
    shape = (rows, lanes)
    block = lane_block(shape, rows)
    lane = lax.broadcasted_iota(jnp.int32, shape, 1)
    row = lax.broadcasted_iota(jnp.int32, shape, 0)
    diag0, diag1, diag2 = lane == row, lane == row + rows, lane == row + 2 * rows
    upper = jnp.logical_and(lane == row + rows + 1, block == 1)
    lower = jnp.logical_and(lane == row + rows - 1, block == 1)
    load_lane = jnp.logical_and(lane >= 3 * rows, lane < 3 * rows + maps)
    tops, bottoms = [], []
    for j in range(count):
        f = fields_ref[j]
        above = jnp.where(row == 0, 0.0, pltpu.roll(f, 1, 0))
        h = jnp.broadcast_to(f[:, 0:1], shape)
        v = jnp.broadcast_to(f[:, 1:2], shape)
        w = jnp.broadcast_to(f[:, 2:3], shape)
        va = jnp.broadcast_to(above[:, 1:2], shape)
        flux_above = pltpu.roll(above, 2 * rows, 1)
        along = pltpu.roll(f, rows, 1)
        tops.append(
            jnp.where(diag1, h + va + v + w, 0.0)
            - jnp.where(upper, v, 0.0)
            - jnp.where(lower, va, 0.0)
            - jnp.where(diag2, h, 0.0)
            + jnp.where(load_lane, f + flux_above, 0.0)
        )
        bottoms.append(
            jnp.where(diag1, h, 0.0) - jnp.where(diag0, h, 0.0) + jnp.where(load_lane, along, 0.0)
        )
    return tops, bottoms


def compose(maps_in, x, east, rows):
    block = lane_block(maps_in.shape, rows)
    x = jnp.where(lane_block(x.shape, rows) == 1, 0.0, x)
    zero = jnp.zeros_like(x)
    right = jnp.concatenate([jnp.where(east, x, 0.0), zero, jnp.where(east, 0.0, x), zero], axis=0)
    return jnp.where(block == jnp.where(east, 0, 2), 0.0, maps_in) - product(maps_in, right)


def local_maps(local_ref, width, rows, lanes):
    row = lax.broadcasted_iota(jnp.int32, (rows, lanes), 0)
    lane = lax.broadcasted_iota(jnp.int32, (rows, lanes), 1)
    stacks = [jnp.where(lane == row, -1.0, 0.0)] * width
    position = 0
    while len(stacks) > 1:
        merged = []
        for i in range(len(stacks) // 2):
            x = local_ref[position]
            position += 1
            west = compose(stacks[2 * i], x, False, rows)
            east = compose(stacks[2 * i + 1], x, True, rows)
            merged.append(jnp.concatenate([west, east], axis=0))
        stacks = merged
    return stacks[0]


def partner_of(axis, step):
    me = lax.axis_index(axis)
    side = (me // (1 << step)) % 2
    return me + (1 - 2 * side) * (1 << step), side


def swap_blocks(axis, source_ref, target_ref, send, recv):
    count, me = lax.axis_size(axis), lax.axis_index(axis)
    copies = []
    for step in range(1, count):
        peer = (me + step) % count
        copy = pltpu.make_async_remote_copy(
            src_ref=source_ref.at[peer],
            dst_ref=target_ref.at[me],
            send_sem=send.at[step - 1],
            recv_sem=recv.at[step - 1],
            device_id={axis: peer},
            device_id_type=pl.DeviceIdType.MESH,
        )
        copy.start()
        copies.append(copy)
    target_ref[me] = source_ref[me]
    for copy in copies:
        copy.wait()


def solve_kernel(
    parts_ref, out_ref, got_ref, fields_ref, local_ref, path_ref, mine_ref, theirs_ref, done_ref,
    send_in, recv_in, send_merge, recv_merge, send_out, recv_out, *, rows, maps, strip_steps, panel_steps,
):
    strips, me = lax.axis_size("strip"), lax.axis_index("strip")
    width, _, lanes = fields_ref.shape
    local_rows = rows // strips
    hops = [("strip", s) for s in range(strip_steps)] + [("panel", s) for s in range(panel_steps)]
    barrier = pltpu.get_barrier_semaphore()
    greeted = [("strip", (me + s) % strips) for s in range(1, strips)]
    greeted += [("panel", partner_of("panel", s)[0]) for s in range(panel_steps)]
    for axis, peer in greeted:
        pl.semaphore_signal(barrier, inc=1, device_id={axis: peer}, device_id_type=pl.DeviceIdType.MESH)
    pl.semaphore_wait(barrier, len(greeted))

    swap_blocks("strip", parts_ref, got_ref, send_in, recv_in)
    for s in range(strips):
        for j in range(width):
            fields_ref[j, s * local_rows : (s + 1) * local_rows] = got_ref[
                s, j * local_rows : (j + 1) * local_rows
            ]
    tops, bottoms = load_segments(fields_ref, rows, maps)
    top, bottom = merge_tree(tops, bottoms, rows, local_ref)
    for level, (axis, step) in enumerate(hops):
        partner, side = partner_of(axis, step)
        mine_ref[level, 0] = top
        mine_ref[level, 1] = bottom
        copies = []
        for order, half in enumerate((1 - side, side)):
            copy = pltpu.make_async_remote_copy(
                src_ref=mine_ref.at[level, half],
                dst_ref=theirs_ref.at[level, half],
                send_sem=send_merge.at[level, order],
                recv_sem=recv_merge.at[level, order],
                device_id={axis: partner},
                device_id_type=pl.DeviceIdType.MESH,
            )
            copy.start()
            copies.append(copy)
        east = side == 1
        if level == 0:
            path_ref[...] = local_maps(local_ref, width, rows, lanes)
        else:
            path_ref[...] = compose(path_ref[...], *last, rows)
        copies[0].wait()
        facing = jnp.where(east, top, bottom) + theirs_ref[level, side]
        solved = eliminate_column([facing], rows, rows // 2)
        last = (solved[0], east)
        copies[1].wait()
        far = theirs_ref[level, 1 - side]
        new_tops, new_bottoms = reduce_segments(
            solved, [jnp.where(east, far, top)], [jnp.where(east, bottom, far)], rows
        )
        top, bottom = new_tops[0], new_bottoms[0]

    block = lane_block((rows, lanes), rows)
    wrap = pltpu.roll(top, lanes - rows, 1) + pltpu.roll(bottom, rows, 1)
    closing = top + bottom + jnp.where(block == 1, wrap, 0.0)
    first = eliminate_column([closing], rows, rows // 2)[0]
    first = jnp.where(block == 3, first, 0.0)
    zero = jnp.zeros_like(first)
    maps_all = compose(path_ref[...], *last, rows)
    values = maps_all - product(maps_all, jnp.concatenate([first, zero, first, zero], axis=0))
    slot = lax.broadcasted_iota(jnp.int32, (rows, lanes), 1) // maps
    packed = jnp.zeros((rows, lanes), jnp.float32)
    for j in range(width):
        moved = pltpu.roll(values[j * rows : (j + 1) * rows], (j * maps + rows) % lanes, 1)
        packed = jnp.where(slot == j, moved, packed)
    for s in range(strips):
        done_ref[s] = packed[s * local_rows : (s + 1) * local_rows]
    swap_blocks("strip", done_ref, out_ref, send_out, recv_out)


def power_of_two(n):
    return n >= 2 and n & (n - 1) == 0


def longitude_shards(h_cond, v_cond, confidence, teacher, grad_x, grad_y):
    local_rows, slice_cols = h_cond.shape
    maps = teacher.shape[0]
    strips, panels = lax.axis_size("strip"), lax.axis_size("panel")
    rows, lanes, width = local_rows * strips, 4 * local_rows * strips, slice_cols // strips
    strip_steps, panel_steps = strips.bit_length() - 1, panels.bit_length() - 1
    levels = strip_steps + panel_steps
    along = h_cond[None] * grad_x
    flux = v_cond[None] * grad_y
    load = confidence[None] * teacher - along - flux
    small = jnp.stack([h_cond, v_cond, confidence], axis=0)

    def padded(part):
        return jnp.pad(part, ((0, rows - part.shape[0]), (0, 0), (0, 0)))

    packed = jnp.concatenate([padded(small), padded(flux), padded(along), padded(load)], axis=0)
    packed = jnp.transpose(packed, (2, 1, 0)).reshape(strips, width * local_rows, lanes)
    f32 = jnp.float32
    dma = pltpu.SemaphoreType.DMA
    values = pl.pallas_call(
        functools.partial(
            solve_kernel, rows=rows, maps=maps, strip_steps=strip_steps, panel_steps=panel_steps
        ),
        out_shape=jax.ShapeDtypeStruct((strips, local_rows, lanes), f32),
        in_specs=[pl.BlockSpec(memory_space=pltpu.VMEM)],
        out_specs=pl.BlockSpec(memory_space=pltpu.VMEM),
        scratch_shapes=[
            pltpu.VMEM((strips, width * local_rows, lanes), f32),
            pltpu.VMEM((width, rows, lanes), f32),
            pltpu.VMEM((width - 1, rows, lanes), f32),
            pltpu.VMEM((width * rows, lanes), f32),
            pltpu.VMEM((levels, 2, rows, lanes), f32),
            pltpu.VMEM((levels, 2, rows, lanes), f32),
            pltpu.VMEM((strips, local_rows, lanes), f32),
            dma((strips - 1,)),
            dma((strips - 1,)),
            dma((levels, 2)),
            dma((levels, 2)),
            dma((strips - 1,)),
            dma((strips - 1,)),
        ],
        compiler_params=pltpu.CompilerParams(collective_id=0, has_side_effects=True),
    )(packed)
    values = values[:, :, : width * maps].reshape(strips, local_rows, width, maps)
    return jnp.transpose(values, (3, 1, 0, 2)).reshape(maps, local_rows, slice_cols)


def shards(h_cond, v_cond, confidence, teacher, grad_x, grad_y):
    strips, panels = lax.axis_size("strip"), lax.axis_size("panel")
    rows, cols = h_cond.shape[0] * strips, h_cond.shape[1]
    width = cols // strips
    short = 4 * rows == 128 and 3 <= rows and teacher.shape[0] <= rows and width * teacher.shape[0] <= 4 * rows
    even = cols % strips == 0 and all(power_of_two(n) for n in (strips, panels, width))
    body = longitude_shards if short and even else latitude_shards
    return body(h_cond, v_cond, confidence, teacher, grad_x, grad_y)


def solution(mesh):
    in_specs = (
        P("strip", "panel"),
        P("strip", "panel"),
        P("strip", "panel"),
        P(None, "strip", "panel"),
        P(None, "strip", "panel"),
        P(None, "strip", "panel"),
    )
    out_specs = P(None, "strip", "panel")
    return jax.shard_map(shards, mesh=mesh, in_specs=in_specs, out_specs=out_specs, check_vma=False)
```
